32 devices in a mesh: tm: 8 (over z, x), coef: 4 (over y, core).
Axes of the slice: x: 2, y: 2, z: 4, core: 2. Of those that a mesh axis runs over, the one named last changes fastest.
Arguments:
- design: float32 [6144, 16384], P('tm', 'coef'), may hold values from -6 to 6
- taps: float32 [384], replicated, may hold values from -0.3125 to 0.3125
Outputs:
- coeffs: float32 [256, 16384], P(None, 'coef')
- reduced: float32 [6144, 16384], P('tm', 'coef')
The draws below stay inside these ranges and needn't reach their ends.
All inputs are finite; a program needn't handle non-finite values.
Results may differ from the reference program's by a relative error of at most 0.0003.
Values sent between devices are 32-bit elements; how exact they have to be, the bound alone decides.
No kernel may reach another device: no remote copies, remote signals or barrier semaphores. Data moves between devices by JAX's collectives and lax.ppermute only.
A program may use at most 128 MiB of HBM per device.

```python
import jax
import jax.numpy as jnp
from jax import lax

COLS = 16384
TAPS = 384
PANEL = 256
ROWS_DEV = 768
TIME = 6144
N_TM = 8


def steps_of(stream_key, dims, shards, low, top_value):
    factor_of = 1.0
    for axis_at, parts in shards:
        steps = jax.random.uniform(jax.random.fold_in(jax.random.fold_in(stream_key, 6), axis_at), (parts,), jnp.float32, low / len(shards), top_value / len(shards))
        factor_of = factor_of * jnp.repeat(jnp.exp(steps), dims[axis_at] // parts).reshape((-1,) + (1,) * (len(dims) - 1 - axis_at))
    return factor_of


def normal_values(key, dims, spread, limit, split=(), kind=jnp.bfloat16):
    entries = jax.random.normal(key, dims, jnp.float32) * spread
    if len(split) > 0:
        entries = steps_of(key, dims, split, -0.22, 0.18) * entries
    return jnp.clip(entries, min=-limit, max=limit).astype(kind)


def setup_inputs(seed: int = 0) -> dict:
    arg_keys = jax.random.split(jax.random.key(seed), 3)
    return {
        "design": normal_values(arg_keys[0], (TIME, COLS), 1.0, 6.0, ((0, 8), (1, 4)), jnp.float32),
        "taps": normal_values(arg_keys[1], (TAPS,), TAPS ** -0.5, 0.3125, (), jnp.float32),
    }


def solve_lower(lower, right):
    return lax.linalg.triangular_solve(lower, right, left_side=True, lower=True)

def toeplitz_matrix(taps, height):
    count = taps.shape[0]
    span = height + count - 1
    pattern = jnp.concatenate([taps[::-1], jnp.zeros((span + 1 - count,), taps.dtype)])
    repeated = jnp.tile(pattern, height)
    return repeated[:height * span].reshape(height, span)

def reference(design, taps):
    extra = TAPS - 1
    matrix = toeplitz_matrix(taps, ROWS_DEV)
    padded = jnp.concatenate([jnp.zeros((extra, COLS), jnp.float32), design], axis=0)

    def block(index):
        start = (index * ROWS_DEV).astype(jnp.int32)
        rows = lax.dynamic_slice_in_dim(padded, start, ROWS_DEV + extra, 0)
        return jnp.dot(matrix.astype(jnp.float32), rows.astype(jnp.float32), precision=lax.Precision.HIGHEST, preferred_element_type=jnp.float32)
    white = lax.map(block, jnp.arange(N_TM, dtype=jnp.int32)).reshape(TIME, COLS)
    panel = white[:, :PANEL]
    gram = jnp.dot(panel.T.astype(jnp.float32), panel.astype(jnp.float32), precision=lax.Precision.HIGHEST, preferred_element_type=jnp.float32)
    lower = jnp.linalg.cholesky(gram)
    cross = jnp.dot(panel.T.astype(jnp.float32), white.astype(jnp.float32), precision=lax.Precision.HIGHEST, preferred_element_type=jnp.float32)
    coeffs = solve_lower(lower, cross)
    basis = solve_lower(lower, panel.T).T
    reduced = white - jnp.dot(basis.astype(jnp.float32), coeffs.astype(jnp.float32), precision=lax.Precision.HIGHEST, preferred_element_type=jnp.float32)
    reduced = reduced.at[:, :PANEL].set(jnp.sqrt(jnp.float32(TIME)) * basis)
    return (coeffs, reduced)
```

```python
import functools

import jax
import jax.numpy as jnp
from jax import lax
from jax.experimental import pallas as pl
from jax.experimental.pallas import tpu as pltpu
from jax.sharding import PartitionSpec as P

PANEL = 256
TILE = 512


def exact(left, right):
    return jnp.dot(left, right, precision=lax.Precision.HIGHEST, preferred_element_type=jnp.float32)


def halves(x):
    high = x.astype(jnp.bfloat16)
    low = (x - high.astype(jnp.float32)).astype(jnp.bfloat16)
    return high, low


def outer_halves(x):
    rounded = lax.reduce_precision(x, 8, 7)
    return rounded.astype(jnp.bfloat16), (x - rounded).astype(jnp.bfloat16)


def left_parts(x):
    high, low = outer_halves(x)
    return jnp.concatenate([high, high, low], axis=1)


def right_parts(x):
    high, low = halves(x)
    return jnp.concatenate([high, low, high], axis=0)


def product3(left3, right3):
    return jnp.dot(left3, right3, preferred_element_type=jnp.float32)


def filter_band(taps, rows, before):
    count = taps.shape[0]
    span = rows + before
    pattern = jnp.concatenate([taps[::-1], jnp.zeros((span + 1 - count,), taps.dtype)])
    shift = before - (count - 1)
    pattern = jnp.roll(pattern, shift)
    repeated = jnp.tile(pattern, rows)
    return repeated[: rows * span].reshape(rows, span)


def white_kernel(tile, height, extra, band_ref, design_ref, out_ref):
    for start in range(0, height, tile):
        first = max(0, start - extra)
        window = right_parts(design_ref[first : start + tile, :])
        skipped = first - (start - extra)
        depth = start + tile - first
        high = band_ref[0, :, skipped : skipped + depth]
        low = band_ref[1, :, skipped : skipped + depth]
        left = jnp.concatenate([high, high, low], axis=1)
        out_ref[start : start + tile, :] = product3(left, window)


def own_white(band, design, tile):
    height, width = design.shape
    extra = band.shape[1] - tile
    high, low = outer_halves(band)
    bands = jnp.stack([high, low])
    return pl.pallas_call(
        functools.partial(white_kernel, tile, height, extra),
        grid=(width // TILE,),
        in_specs=[
            pl.BlockSpec(bands.shape, lambda j: (0, 0, 0)),
            pl.BlockSpec((height, TILE), lambda j: (0, j)),
        ],
        out_specs=pl.BlockSpec((height, TILE), lambda j: (0, j)),
        out_shape=jax.ShapeDtypeStruct((height, width), jnp.float32),
        cost_estimate=pl.CostEstimate(
            flops=6 * height * (tile + extra) * width, bytes_accessed=8 * height * width, transcendentals=0
        ),
        name="own_white",
    )(bands, design)


def cross_kernel(left_ref, design_ref, out_ref):
    out_ref[...] = product3(left_ref[...], right_parts(design_ref[...]))


def cross_sums(weights, design):
    height, width = design.shape
    left = left_parts(weights.T)
    return pl.pallas_call(
        cross_kernel,
        grid=(width // TILE,),
        in_specs=[
            pl.BlockSpec(left.shape, lambda j: (0, 0)),
            pl.BlockSpec((height, TILE), lambda j: (0, j)),
        ],
        out_specs=pl.BlockSpec((PANEL, TILE), lambda j: (0, j)),
        out_shape=jax.ShapeDtypeStruct((PANEL, width), jnp.float32),
        cost_estimate=pl.CostEstimate(
            flops=6 * height * PANEL * width, bytes_accessed=4 * height * width, transcendentals=0
        ),
        name="cross_sums",
    )(left, design)


def final_kernel(
    flag_ref, inverse_ref, basis_ref, upper_ref, scaled_ref, cross_ref, white_ref, halo_ref, coeffs_ref, out_ref
):
    extra = halo_ref.shape[0]
    coeffs = product3(inverse_ref[...], right_parts(cross_ref[...]))
    coeffs_ref[...] = coeffs
    out_ref[...] = white_ref[...] - product3(basis_ref[...], right_parts(coeffs))
    out_ref[0:extra, :] += product3(upper_ref[...], right_parts(halo_ref[...]))

    @pl.when((flag_ref[0] == 1) & (pl.program_id(0) == 0))
    def _():
        out_ref[:, 0:PANEL] = scaled_ref[...]


def finish(first_block, inverse, basis, upper, scaled, cross, white, halo):
    height, width = white.shape
    extra = halo.shape[0]
    fixed = lambda a: pl.BlockSpec(a.shape, lambda j, flag: (0, 0))
    column = lambda rows: pl.BlockSpec((rows, TILE), lambda j, flag: (0, j))
    inverse, basis, upper = left_parts(inverse), left_parts(basis), left_parts(upper)
    return pl.pallas_call(
        final_kernel,
        grid_spec=pltpu.PrefetchScalarGridSpec(
            num_scalar_prefetch=1,
            grid=(width // TILE,),
            in_specs=[
                fixed(inverse), fixed(basis), fixed(upper), fixed(scaled), column(PANEL), column(height), column(extra)
            ],
            out_specs=[column(PANEL), column(height)],
        ),
        out_shape=[
            jax.ShapeDtypeStruct((PANEL, width), jnp.float32),
            jax.ShapeDtypeStruct((height, width), jnp.float32),
        ],
        cost_estimate=pl.CostEstimate(
            flops=6 * width * (height * PANEL + PANEL * PANEL + extra * extra),
            bytes_accessed=4 * width * (2 * height + extra + 2 * PANEL),
            transcendentals=0,
        ),
        name="finish",
    )(first_block, inverse, basis, upper, scaled, cross, white, halo)


def filter_rows(band, extended, rows, tile):
    span = band.shape[1]
    pieces = []
    for start in range(0, rows, tile):
        size = min(tile, rows - start)
        window = extended[start : start + span - (tile - size)]
        pieces.append(exact(band[:size, : span - (tile - size)], window))
    return jnp.concatenate(pieces, axis=0)


def correlate_rows(band, ahead, rows, tile):
    span = band.shape[1]
    flipped = band[::-1, ::-1]
    pieces = []
    for start in range(0, rows, tile):
        pieces.append(exact(flipped, ahead[start : start + span]))
    return jnp.concatenate(pieces, axis=0)


def broadcast_from_first(value, axis):
    count = lax.axis_size(axis)
    index = lax.axis_index(axis)
    distance = count // 2
    while distance >= 1:
        route = [(i, i + distance) for i in range(0, count, 2 * distance)]
        received = lax.ppermute(value, axis, route)
        value = jnp.where(index % (2 * distance) == distance, received, value)
        distance //= 2
    return value


def per_device(design, taps):
    height, width = design.shape
    count = taps.shape[0]
    extra = count
    steps = lax.axis_size("tm")
    columns = lax.axis_size("coef")
    index = lax.axis_index("tm")
    total_rows = height * steps
    tile = 256
    band = filter_band(taps, tile, extra)

    raw = design[:, :PANEL]
    up = [(i * columns, (i + 1) * columns) for i in range(steps - 1)]
    down = [(b, a) for a, b in up]
    behind = lax.ppermute(raw[height - extra :], ("tm", "coef"), up)
    ahead = lax.ppermute(raw[:extra], ("tm", "coef"), down)
    halo = lax.ppermute(design[height - extra :], "tm", [(i, i + 1) for i in range(steps - 1)])

    extended = jnp.concatenate([behind, raw, ahead], axis=0)
    filtered = filter_rows(band, extended, height + extra, tile)
    panel = filtered[:height]
    following = jnp.where(index < steps - 1, filtered[height:], 0.0)
    weights = correlate_rows(band, jnp.concatenate([panel, following], axis=0), height, tile)
    gram = exact(panel.T, panel)
    distance = 1
    while distance < steps:
        route = [(i * columns, (i ^ distance) * columns) for i in range(steps)]
        gram = gram + lax.ppermute(gram, ("tm", "coef"), route)
        distance *= 2

    weights = broadcast_from_first(weights, "coef")
    both = broadcast_from_first(jnp.concatenate([panel, gram], axis=0), "coef")
    panel, gram = both[:height], both[height:]

    white = own_white(band, design, tile)
    cross = lax.psum(cross_sums(weights, design), "tm")

    lower = jnp.linalg.cholesky(gram)
    inverse = lax.linalg.triangular_solve(
        lower, jnp.eye(PANEL, dtype=jnp.float32), left_side=True, lower=True
    )
    basis = exact(panel, inverse.T)
    scaled = jnp.sqrt(jnp.float32(total_rows)) * basis
    upper = filter_band(taps, extra, extra)[:, :extra]
    first_block = (lax.axis_index("coef") == 0).astype(jnp.int32).reshape(1)
    coeffs, reduced = finish(first_block, inverse, basis, upper, scaled, cross, white, halo)
    return coeffs, reduced


def solution(mesh):
    in_specs = (P("tm", "coef"), P())
    out_specs = (P(None, "coef"), P("tm", "coef"))
    return jax.shard_map(
        per_device, mesh=mesh, in_specs=in_specs, out_specs=out_specs, check_vma=False
    )
```

```python
import functools

import jax
import jax.numpy as jnp
from jax import lax
from jax.experimental import pallas as pl
from jax.experimental.pallas import tpu as pltpu
from jax.sharding import PartitionSpec as P

PANEL = 256
TILE = 512
CHUNKS = 8


def exact(left, right):
    return jnp.dot(left, right, precision=lax.Precision.HIGHEST, preferred_element_type=jnp.float32)


def exact_t(left, right):
    return lax.dot_general(
        left, right, (((0,), (0,)), ((), ())), precision=lax.Precision.HIGHEST, preferred_element_type=jnp.float32
    )


def halves(x):
    high = x.astype(jnp.bfloat16)
    low = (x - high.astype(jnp.float32)).astype(jnp.bfloat16)
    return high, low


def right_parts(x):
    high, low = halves(x)
    return jnp.concatenate([high, low, high], axis=0)


def product3(left3, right3):
    return jnp.dot(left3, right3, preferred_element_type=jnp.float32)


ANY = pl.BlockSpec(memory_space=pl.ANY)


def call(kernel, name, grid, blocks, arrays, outs, out_blocks, flops, aliases=None, scalars=(), scratch=()):
    moved = sum(8 * o.shape[0] * b.block_shape[-1] * max(grid) for o, b in zip(outs, out_blocks))
    return pl.pallas_call(
        kernel,
        grid_spec=pltpu.PrefetchScalarGridSpec(
            num_scalar_prefetch=len(scalars), grid=grid, in_specs=blocks, out_specs=out_blocks, scratch_shapes=scratch
        ),
        out_shape=outs,
        input_output_aliases=aliases or {},
        cost_estimate=pl.CostEstimate(flops=int(flops), bytes_accessed=int(moved), transcendentals=0),
        name=name,
    )(*scalars, *arrays)


def whole_block(a):
    return pl.BlockSpec(a.shape, lambda *_: (0,) * len(a.shape))


def shaped(shape, dtype=jnp.float32):
    return jax.ShapeDtypeStruct(shape, dtype)


def slide(row, rows):
    return pltpu.roll(jnp.broadcast_to(row, (rows, row.shape[1])), 0, 1, stride=1, stride_axis=0)


def tables_kernel(back_ref, forward_ref, band_ref, turned_ref, bands_ref, upper_ref):
    tile, span = band_ref.shape
    extra = upper_ref.shape[0]
    band = slide(back_ref[:, :span], tile)
    band_ref[...] = band
    turned_ref[...] = slide(forward_ref[:, :span], tile)
    bands_ref[0], bands_ref[1] = halves(band)
    high, low = halves(slide(back_ref[...], extra)[:, :extra])
    upper_ref[...] = jnp.concatenate([high, high, low], axis=1)


def tables(taps, tile):
    count = taps.shape[0]
    back = jnp.concatenate([jnp.zeros((1,)), taps[::-1], jnp.zeros((count - 1,))]).reshape(1, 2 * count)
    forward = jnp.concatenate([taps, jnp.zeros((count,))]).reshape(1, 2 * count)
    outs = [
        shaped((tile, tile + count)),
        shaped((tile, tile + count)),
        shaped((2, tile, tile + count), jnp.bfloat16),
        shaped((count, 3 * count), jnp.bfloat16),
    ]
    return call(
        tables_kernel, "tables", (1,), [whole_block(back)] * 2, [back, forward], outs, [whole_block(o) for o in outs], 0
    )


def edges_kernel(raw_ref, first_ref, last_ref):
    extra = first_ref.shape[0]
    first_ref[...] = raw_ref[:extra, :]
    last_ref[...] = raw_ref[raw_ref.shape[0] - extra :, :]


def edges(design, extra):
    height = design.shape[0]
    outs = [shaped((extra, PANEL))] * 2
    return call(
        edges_kernel,
        "edges",
        (1,),
        [pl.BlockSpec((height, PANEL), lambda j: (0, 0))],
        [design],
        outs,
        [whole_block(o) for o in outs],
        0,
    )


def cut_kernel(rows_ref, token_ref, out_ref):
    out_ref[...] = rows_ref[...]


def cut(design, extra, first, chunk, token):
    height = design.shape[0]
    tile = min(PANEL, chunk)
    return call(
        cut_kernel,
        "cut",
        (chunk // tile,),
        [pl.BlockSpec((extra, tile), lambda j: (height // extra - 1, first // tile + j)), ANY],
        [design, token],
        [shaped((extra, chunk))],
        [pl.BlockSpec((extra, tile), lambda j: (0, j))],
        0,
    )[0]


def panel_kernel(
    last_ref, band_ref, turned_ref, behind_ref, raw_ref, ahead_ref, weights_ref, panel_ref, gram_ref, rows_ref, done_ref
):
    height, extra = raw_ref.shape[0], behind_ref.shape[0]
    tile = band_ref.shape[0]
    rows_ref[:extra, :] = behind_ref[...]
    rows_ref[extra : extra + height, :] = raw_ref[...]
    rows_ref[extra + height :, :] = ahead_ref[...]
    for start in range(0, height + extra, tile):
        size = min(tile, height + extra - start)
        done_ref[start : start + size, :] = exact(
            band_ref[:size, : extra + size], rows_ref[start : start + extra + size, :]
        )

    @pl.when(last_ref[0] == 1)
    def _():
        done_ref[height:, :] = jnp.zeros((extra, done_ref.shape[1]), jnp.float32)

    for start in range(0, height, tile):
        weights_ref[start : start + tile, :] = exact(turned_ref[...], done_ref[start : start + tile + extra, :])
    panel_ref[...] = done_ref[:height, :]
    gram_ref[...] = exact_t(done_ref[:height, :], done_ref[:height, :])


def filter_panel(last, band, turned, behind, design, ahead):
    height, extra = design.shape[0], behind.shape[0]
    outs = [shaped((height, PANEL)), shaped((height, PANEL)), shaped((PANEL, PANEL))]
    return call(
        panel_kernel,
        "filter_panel",
        (1,),
        [whole_block(band), whole_block(turned), whole_block(behind)]
        + [pl.BlockSpec((height, PANEL), lambda *_: (0, 0)), whole_block(ahead)],
        [band, turned, behind, design, ahead],
        outs,
        [whole_block(o) for o in outs],
        4 * 10**9,
        scalars=(last,),
        scratch=[pltpu.VMEM((height + 2 * extra, PANEL), jnp.float32), pltpu.VMEM((height + extra, PANEL), jnp.float32)],
    )


def white_kernel(tile, bands_ref, design_ref, token_ref, out_ref):
    height = design_ref.shape[0]
    extra = bands_ref.shape[2] - tile
    for start in range(0, height, tile):
        first = max(0, start - extra)
        window = right_parts(design_ref[first : start + tile, :])
        skipped = first - (start - extra)
        high, low = bands_ref[0, :, skipped:], bands_ref[1, :, skipped:]
        out_ref[start : start + tile, :] = product3(jnp.concatenate([high, high, low], axis=1), window)


def own_white(bands, design, token):
    height, width = design.shape
    tile = bands.shape[1]
    column = pl.BlockSpec((height, TILE), lambda j: (0, j))
    return call(
        functools.partial(white_kernel, tile),
        "own_white",
        (width // TILE,),
        [whole_block(bands), column, ANY],
        [bands, design, token],
        [shaped((height, width))],
        [column],
        6 * height * (tile + bands.shape[2]) // 2 * width,
    )[0]


def turn_kernel(pick_ref, own_ref, other_ref, out_ref):
    value = jnp.where(pick_ref[0] == 1, other_ref[...], own_ref[...]).T
    high, low = halves(value)
    out_ref[...] = jnp.concatenate([high, high, low], axis=1)


def turn(pick, own, other):
    out = shaped((PANEL, 3 * own.shape[0]), jnp.bfloat16)
    return call(
        turn_kernel, "turn", (1,), [whole_block(own)] * 2, [own, other], [out], [whole_block(out)], 0, scalars=(pick,)
    )[0]


def cross_kernel(count, blocks_ref, left_ref, design_ref, *out_refs):
    for i in range(count):

        @pl.when(pl.program_id(0) == i)
        def _(i=i):
            out_refs[i][...] = product3(left_ref[...], right_parts(design_ref[...]))


def cross_sums(left, design, blocks, segment, count):
    height = design.shape[0]
    return call(
        functools.partial(cross_kernel, count),
        "cross_sums",
        (count,),
        [whole_block(left), pl.BlockSpec((height, segment), lambda j, at: (0, at[j]))],
        [left, design],
        [shaped((PANEL, segment))] * count,
        [pl.BlockSpec((PANEL, segment), lambda j, at: (0, 0))] * count,
        6 * height * PANEL * segment * count,
        scalars=(blocks,),
    )


def halo_kernel(skip, info_ref, upper_ref, near_ref, far_ref, white_ref, out_ref):
    rows = near_ref[...]
    if far_ref is not None:
        rows = jnp.where(info_ref[1] == 1, far_ref[...], rows)
    added = white_ref[...] + product3(upper_ref[...], right_parts(rows))
    if skip:
        keep = (info_ref[0] == 1) & (pl.program_id(0) * out_ref.shape[1] < PANEL)
        added = jnp.where(keep, white_ref[...], added)
    out_ref[...] = added


def add_halo(white, upper, halo, start, info):
    near, far = halo
    extra, chunk = near.shape
    tile = min(PANEL, chunk)
    first = start // tile
    column = pl.BlockSpec((extra, tile), lambda j, info: (0, j))
    place = pl.BlockSpec((extra, tile), lambda j, info: (0, first + j))
    halos = [near] if far is None else [near, far]

    def kernel(info_ref, upper_ref, near_ref, *refs):
        far_ref = None if far is None else refs[0]
        halo_kernel(start < PANEL, info_ref, upper_ref, near_ref, far_ref, *refs[-2:])

    return call(
        kernel,
        "add_halo",
        (chunk // tile,),
        [whole_block(upper)] + [column] * len(halos) + [place],
        [upper, *halos, white],
        [shaped(white.shape)],
        [place],
        6 * extra * extra * chunk,
        aliases={2 + len(halos): 0},
        scalars=(info,),
    )[0]


def reduce_kernel(count, tiles, first_call, place_ref, inverse_ref, basis_ref, scaled_ref, *refs):
    crosses = refs[:count]
    white_ref = refs[count]
    coeffs_ref, out_ref = refs[-2:]
    step = pl.program_id(0)
    for i in range(count):

        @pl.when(step // tiles == i)
        def _(i=i):
            coeffs = product3(inverse_ref[...], right_parts(crosses[i][...]))
            coeffs_ref[...] = coeffs
            out_ref[...] = white_ref[...] - product3(basis_ref[...], right_parts(coeffs))

    @pl.when((place_ref[0] == 1) & (place_ref[1 + step // tiles] * tiles + step % tiles < PANEL // out_ref.shape[1]))
    def _():
        out_ref[...] = scaled_ref[...]


def reduce_segments(white, coeffs, tables, crosses, place):
    inverse, basis, scaled = tables
    height, width = white.shape
    count, segment = len(crosses), crosses[0].shape[1]
    tile = min(PANEL, segment)
    tiles = segment // tile
    last = PANEL // tile - 1
    at = lambda j, place: place[1 + j // tiles] * tiles + j % tiles
    column = lambda rows: pl.BlockSpec((rows, tile), lambda j, place: (0, at(j, place)))
    source = lambda i: pl.BlockSpec((PANEL, tile), lambda j, place: (0, jnp.clip(j - i * tiles, 0, tiles - 1)))
    first_call = coeffs is None
    arrays = [inverse, basis, scaled, *crosses, white] + ([] if first_call else [coeffs])
    aliases = {4 + count: 1}
    if not first_call:
        aliases[5 + count] = 0
    return call(
        functools.partial(reduce_kernel, count, tiles, first_call),
        "reduce_segments",
        (count * tiles,),
        [
            whole_block(inverse),
            whole_block(basis),
            pl.BlockSpec((height, tile), lambda j, place: (0, jnp.minimum(at(j, place), last))),
        ]
        + [source(i) for i in range(count)]
        + [column(height)]
        + ([] if first_call else [ANY]),
        arrays,
        [shaped((PANEL, width)), shaped((height, width))],
        [column(PANEL), column(height)],
        6 * segment * count * (height * PANEL + PANEL * PANEL),
        aliases=aliases,
        scalars=(place,),
    )


STEP = 32


def eliminate(block):
    size = block.shape[0]
    both = jnp.concatenate([block, jnp.eye(size, dtype=jnp.float32)], axis=1)
    rows = lax.broadcasted_iota(jnp.int32, (size, 1), 0)
    for j in range(size - 1):
        factor = jnp.where(rows > j, both[:, j : j + 1] / both[j : j + 1, j : j + 1], 0.0)
        both = both - factor * both[j : j + 1, :]
    on_diagonal = lax.broadcasted_iota(jnp.int32, (size, size), 0) == lax.broadcasted_iota(
        jnp.int32, (size, size), 1
    )
    diagonal = jnp.sum(jnp.where(on_diagonal, both[:, :size], 0.0), axis=1, keepdims=True)
    return both[:, size:] / jnp.sqrt(diagonal)


def eliminate_rows(work_ref, begin, end):
    size = work_ref.shape[0]
    for start in range(begin, end, STEP):
        stop = start + STEP
        rows = exact(eliminate(work_ref[start:stop, start:stop]), work_ref[start:stop, :])
        work_ref[start:stop, :] = rows
        if stop < size:
            work_ref[stop:, :] = work_ref[stop:, :] - exact_t(rows[:, stop:size], rows)


def factor_kernel(pick_ref, gram_ref, other_ref, token_ref, work_ref):
    size = gram_ref.shape[0]
    work_ref[:, :size] = jnp.where(pick_ref[0] == 1, other_ref[...], gram_ref[...])
    work_ref[:, size:] = (
        lax.broadcasted_iota(jnp.int32, (size, size), 0) == lax.broadcasted_iota(jnp.int32, (size, size), 1)
    ).astype(jnp.float32)
    eliminate_rows(work_ref, 0, size // 2)


def basis_kernel(pick_ref, factor_ref, work_in_ref, panel_ref, other_ref, token_ref, inverse_ref, basis_ref, scaled_ref, work_ref):
    size = work_ref.shape[0]
    work_ref[...] = work_in_ref[...]
    eliminate_rows(work_ref, size // 2, size)
    inverse = work_ref[:, size:]
    panel = jnp.where(pick_ref[0] == 1, other_ref[...], panel_ref[...])
    basis = lax.dot_general(
        panel,
        inverse,
        (((1,), (1,)), ((), ())),
        precision=lax.Precision.HIGHEST,
        preferred_element_type=jnp.float32,
    )
    scaled_ref[...] = factor_ref[0] * basis
    for value, ref in ((inverse, inverse_ref), (basis, basis_ref)):
        high, low = halves(value)
        ref[...] = jnp.concatenate([high, high, low], axis=1)


def half_factor(pick, gram, other, token):
    size = gram.shape[0]
    out = shaped((size, 2 * size))
    return call(
        factor_kernel,
        "half_factor",
        (1,),
        [whole_block(gram)] * 2 + [ANY],
        [gram, other, token],
        [out],
        [whole_block(out)],
        7 * 10**9,
        scalars=(pick,),
    )[0]


def basis_of(pick, scale, work, panel, other, token):
    height = panel.shape[0]
    outs = [shaped((PANEL, 3 * PANEL), jnp.bfloat16), shaped((height, 3 * PANEL), jnp.bfloat16), shaped((height, PANEL))]
    return call(
        basis_kernel,
        "basis",
        (1,),
        [pl.BlockSpec(memory_space=pltpu.SMEM), whole_block(work), whole_block(panel), whole_block(panel), ANY],
        [scale, work, panel, other, token],
        outs,
        [whole_block(o) for o in outs],
        7 * 10**9,
        scalars=(pick,),
        scratch=[pltpu.VMEM((PANEL, 2 * PANEL), jnp.float32)],
    )


def broadcast_from_first(value, axis):
    count = lax.axis_size(axis)
    index = lax.axis_index(axis)
    distance = count // 2
    while distance >= 1:
        route = [(i, i + distance) for i in range(0, count, 2 * distance)]
        received = lax.ppermute(value, axis, route)
        pick = index % (2 * distance) == distance
        if distance == 1:
            return value, received, pick.astype(jnp.int32).reshape(1)
        value = jnp.where(pick, received, value)
        distance //= 2


def bit_of(index, bit):
    return (index >> bit) & 1


class Sum:
    def __init__(self, order, index, first, segment):
        self.bits = max(1, len(order) - len(order) // 2)
        self.order, self.segment = order, segment
        self.count = 1 << self.bits
        key = 0
        for m, bit in enumerate(order[: self.bits]):
            key = key + (bit_of(index, bit) << (self.bits - 1 - m))
        self.blocks = first // segment + jnp.bitwise_xor(jnp.arange(self.count, dtype=jnp.int32), key)


def per_device(design, taps):
    height, width = design.shape
    extra = taps.shape[0]
    size = lax.axis_size("tm")
    columns = lax.axis_size("coef")
    index = lax.axis_index("tm")
    flag = (lax.axis_index("coef") == 0).astype(jnp.int32).reshape(1)

    bits = size.bit_length() - 1
    near = bits // 2
    nx = 1 << near
    low_bits, high_bits = list(range(near)), list(range(near, bits))
    parts = 1 << (bits - near)
    segment = width // (2 * parts)
    kinds = {
        "z": Sum(high_bits + low_bits, index, 0, segment),
        "x": Sum(low_bits + high_bits, index, parts * segment, segment),
    }
    chunk = width // CHUNKS
    chain = [(i, i + 1) for i in range(size - 1)]
    turned_route = [(i, i + 1) for i in range(size) if i % nx != nx - 1]
    turned_route += [(i, i - nx + 1) for i in range(nx - 1, size - nx, nx)]
    onward = [(i, i + nx) for i in range(0, size - nx, nx)]

    halos = []

    def send_halo(token):
        k = len(halos)
        piece = cut(design, extra, k * chunk, chunk, token)
        if k % 2 == 0:
            halos.append((lax.ppermute(piece, "tm", chain), None))
        else:
            first = lax.ppermute(piece, "tm", turned_route)
            halos.append((first, lax.ppermute(first, "tm", onward)))
        return piece

    up = [(i * columns, (i + 1) * columns) for i in range(size - 1)]
    down = [(b, a) for a, b in up]
    first_rows, last_rows = edges(design, extra)
    behind = lax.ppermute(last_rows, ("tm", "coef"), up)
    ahead = lax.ppermute(first_rows, ("tm", "coef"), down)
    send_halo(first_rows)
    band, turned, bands, upper = tables(taps, 256)

    last = (index == size - 1).astype(jnp.int32).reshape(1)
    weights, panel, gram = filter_panel(last, band, turned, behind, design, ahead)
    own, other, pick = broadcast_from_first(weights, "coef")
    send_halo(weights)
    white = own_white(bands, design, weights)
    for bit in high_bits + low_bits:
        route = [(i * columns, (i ^ (1 << bit)) * columns) for i in range(size)]
        gram = gram + lax.ppermute(gram, ("tm", "coef"), route)
    panel, panel_other, _ = broadcast_from_first(panel, "coef")
    gram, gram_other, _ = broadcast_from_first(gram, "coef")

    left = turn(pick, own, other)
    half = parts // 2
    values = {}
    for lo in (half, 0):
        names = [(kind, lo + i) for kind in ("x", "z") for i in range(half)]
        blocks = jnp.concatenate([lax.slice_in_dim(kinds[kind].blocks, lo, lo + half) for kind in ("x", "z")])
        for name, value in zip(names, cross_sums(left, design, blocks, segment, len(names))):
            values[name] = value

    def swap(value, bit):
        return lax.ppermute(value, "tm", [(i, i ^ (1 << bit)) for i in range(size)])

    def scatter(kind, m):
        gap = parts >> (m + 1)
        got = {r: swap(values[kind, r], kinds[kind].order[m]) for r in reversed(range(gap, 2 * gap))}
        for r in reversed(range(gap)):
            values[kind, r] = values[kind, r] + got[r + gap]

    def whole(kind):
        group = kinds[kind]
        for bit in group.order[group.bits :]:
            values[kind, 0] = values[kind, 0] + swap(values[kind, 0], bit)

    def gather(kind, m):
        gap = parts >> (m + 1)
        for r in range(gap):
            values[kind, r + gap] = swap(values[kind, r], kinds[kind].order[m])

    steps = kinds["x"].bits
    kept = values["x", 0]
    scatter("x", 0)
    scatter("z", 0)
    send_halo(kept)
    work = half_factor(pick, gram, gram_other, values["z", half - 1])
    for m in range(1, steps):
        scatter("x", m)
        scatter("z", m)
    send_halo(values["z", 0])
    scale = jnp.sqrt(jnp.float32(height * size)).reshape(1)
    reducers = basis_of(pick, scale, work, panel, panel_other, values["z", 0])
    whole("x")
    whole("z")
    send_halo(values["z", 0])
    for m in reversed(range(steps)):
        gather("x", m)
        gather("z", m)
    send_halo(values["x", half])
    token = values["x", parts - 1]
    while len(halos) < CHUNKS:
        token = send_halo(token)

    info = jnp.concatenate([flag, (index % nx == 0).astype(jnp.int32).reshape(1)])
    coeffs = None

    def halo_in(k):
        return add_halo(white, upper, halos[k], k * chunk, info)

    def reduce_in(kind, lo, hi):
        place = jnp.concatenate([flag, lax.slice_in_dim(kinds[kind].blocks, lo, hi)])
        return reduce_segments(white, coeffs, reducers, [values[kind, r] for r in range(lo, hi)], place)

    for k in range(4):
        white = halo_in(k)
    coeffs, white = reduce_in("x", 0, parts)
    white = halo_in(4)
    coeffs, white = reduce_in("z", 0, half)
    coeffs, white = reduce_in("z", half, parts)
    for k in range(5, CHUNKS):
        white = halo_in(k)
    return coeffs, white


def solution(mesh):
    in_specs = (P("tm", "coef"), P())
    out_specs = (P(None, "coef"), P("tm", "coef"))
    return jax.shard_map(
        per_device, mesh=mesh, in_specs=in_specs, out_specs=out_specs, check_vma=False
    )
```
